256 devices in a mesh: seg: 8 (over x, z_lo), bond: 32 (over z_hi, y, core).
Axes of the slice: x: 4, y: 4, z: 8 (z_hi: 4, z_lo: 2; z = z_hi * 2 + z_lo), core: 2. Of those that a mesh axis runs over, the one named last changes fastest.
Arguments:
- last_sites: bfloat16 [8, 1024, 2048], P('seg', 'bond'), may hold values from -6 to 6
- first_sites: bfloat16 [8, 1024, 2048], P('seg', 'bond'), may hold values from -0.1875 to 0.1875
- start_basis: float32 [2048, 256], replicated, may hold values from -6 to 6
- fields: float32 [8, 2], replicated, may hold values from -3 to 3
- ranks: int32 [8], replicated, may hold values from 128 to 256
Outputs:
- new_left: float32 [8, 2048, 256], P('seg', 'bond')
- new_right: float32 [8, 256, 2048], P('seg')
The draws below stay inside these ranges and needn't reach their ends.
All inputs are finite; a program needn't handle non-finite values.
Results may differ from the reference program's by a relative error of at most 0.00035.
Values may be sent and summed in bfloat16 or wider, within the bound.
A program may use at most 64 MiB of HBM per device.

```python
import jax
import jax.numpy as jnp
from jax import lax

CHI = 1024
KEEP = 256
ITERS = 4
BONDS = 8


def set_ends(entries, own_key, least, top_value):
    index_at = [jax.random.randint(jax.random.fold_in(own_key, axis), (), 0, length) for axis, length in enumerate(entries.shape)]
    main_axis = entries.shape.index(max(entries.shape))
    beside = index_at[:main_axis] + [(index_at[main_axis] + 1) % entries.shape[main_axis]] + index_at[main_axis + 1:]
    return entries.at[tuple(index_at)].set(least).at[tuple(beside)].set(top_value)


def steps_of(rng, extent, pieces, smallest, high):
    def one(dim, shards_of):
        draws = jax.random.uniform(jax.random.fold_in(jax.random.fold_in(rng, 6), dim), (shards_of,), jnp.float32, smallest / len(pieces), high / len(pieces))
        return jnp.repeat(jnp.exp(draws), extent[dim] // shards_of).reshape((-1,) + (1,) * (len(extent) - dim - 1))

    level = one(*pieces[0])
    for cut in pieces[1:]:
        level = level * one(*cut)
    return level


def gaussian(stream_key, shape, scale, most, split=(), kind=jnp.bfloat16):
    loudness = steps_of(stream_key, shape, split, -0.22, 0.18) if split else 1.0
    entries = jax.random.normal(stream_key, shape, jnp.float32) * scale * loudness
    return jnp.minimum(jnp.maximum(entries, -most), most).astype(kind)


def setup_inputs(seed: int = 0) -> dict:
    arg_keys = jax.random.split(jax.random.key(seed), 6)
    last_sites = gaussian(arg_keys[0], (BONDS, CHI, 2 * CHI), 1.0, 6.0, ((0, 8), (1, 32)))
    first_sites = gaussian(arg_keys[1], (BONDS, CHI, 2 * CHI), CHI ** -0.5, 0.1875, ((0, 8), (1, 32)))
    start_basis = gaussian(arg_keys[2], (2 * CHI, KEEP), 1.0, 6.0, (), jnp.float32)
    fields = jnp.clip(jax.random.uniform(arg_keys[3], (BONDS, 2), jnp.float32, -3.0, 3.0), -3.0, 3.0)
    ranks = set_ends(jax.random.randint(arg_keys[4], (BONDS,), KEEP // 2, KEEP + 1), jax.random.fold_in(arg_keys[4], 1), KEEP // 2, KEEP).astype(jnp.int32)
    return {"last_sites": last_sites, "first_sites": first_sites, "start_basis": start_basis, "fields": fields, "ranks": ranks}


time_step = 0.5
anisotropy = 0.6

def bond_gate(pair):
    left_field = pair[0]
    right_field = pair[1]
    half_diff = 0.5 * (left_field - right_field)
    width = jnp.sqrt(half_diff * half_diff + 0.25)
    factor = jnp.exp(time_step * anisotropy / 4.0)
    cosine = jnp.cosh(time_step * width)
    ratio = jnp.sinh(time_step * width) / width
    total = left_field + right_field
    zero = jnp.zeros((), jnp.float32)
    first = jnp.exp(-time_step * (anisotropy / 4.0 + total / 2.0))
    last = jnp.exp(-time_step * (anisotropy / 4.0 - total / 2.0))
    middle = factor * (cosine - half_diff * ratio)
    other = factor * (cosine + half_diff * ratio)
    cross = -factor * ratio * 0.5
    rows = [jnp.stack([first, zero, zero, zero]), jnp.stack([zero, middle, cross, zero]), jnp.stack([zero, cross, other, zero]), jnp.stack([zero, zero, zero, last])]
    return jnp.stack(rows).astype(jnp.float32).reshape(2, 2, 2, 2)

def apply_gate(theta, pair):
    gate = bond_gate(pair)
    rows = theta.shape[0] // 2
    width = theta.shape[1] // 2
    four = theta.reshape(rows, 2, 2, width)
    mixed = jnp.einsum('pqrs,arsc->apqc', gate, four, precision=lax.Precision.HIGHEST)
    return mixed.reshape(rows * 2, width * 2)

def orthonormal(cols, unused):
    gram = jnp.dot(cols.T, cols, precision=lax.Precision.HIGHEST) + jnp.diag(unused)
    chol = jnp.linalg.cholesky(gram)
    return lax.linalg.triangular_solve(chol, cols, left_side=False, lower=True, transpose_a=True)

def one_bond(inputs, start_basis):
    left, right, pair, rank = inputs
    theta = jnp.dot(left.reshape(-1, right.shape[0]).astype(jnp.float32), right.astype(jnp.float32), preferred_element_type=jnp.float32)
    mixed = apply_gate(theta, pair)
    unused = (jnp.arange(start_basis.shape[1], dtype=jnp.int32) >= rank).astype(jnp.float32)
    basis = start_basis * (1.0 - unused)[None, :]
    for step in range(ITERS):
        image = jnp.dot(mixed, basis, precision=lax.Precision.HIGHEST)
        cols = jnp.dot(mixed.T, image, precision=lax.Precision.HIGHEST)
        basis = orthonormal(cols, unused)
    left_factor = jnp.dot(mixed, basis, precision=lax.Precision.HIGHEST)
    right_factor = jnp.sqrt(jnp.float32(mixed.shape[1])) * basis.T
    return (left_factor, right_factor)

def reference(last_sites, first_sites, start_basis, fields, ranks):
    following = jnp.roll(first_sites, -1, axis=0)
    left_all, right_all = lax.map(lambda inputs: one_bond(inputs, start_basis), (last_sites, following, fields, ranks))
    return (left_all, jnp.roll(right_all, 1, axis=0))
```

```python
import functools

import jax
import jax.numpy as jnp
from jax import lax
from jax.experimental import pallas as pl
from jax.experimental.pallas import tpu as pltpu
from jax.sharding import PartitionSpec as P

ITERS = 4
KEEP = 256
CHI = 1024
WIDE = 2048
ROWS = 64
Z, Y, CORES = 4, 4, 2

time_step = 0.5
anisotropy = 0.6
F32 = jnp.float32
BF16 = jnp.bfloat16


def halves(x):
    high = x.astype(BF16)
    return high, (x - high.astype(F32)).astype(BF16)


def dot(a, b, dims):
    return lax.dot_general(a, b, (dims, ((), ())), preferred_element_type=F32)


def splat(x, row, lane):
    return jnp.broadcast_to(x[row : row + 1, lane : lane + 1], (8, 128))


def eliminate_panel(work, factor, start):
    own = start // 128
    tiles = list(range(own, 2)) + [2 + t for t in range(own + 1)]
    sub = lax.broadcasted_iota(jnp.int32, (8, 128), 0)
    groups = 4
    x = [
        {t: work[start + 8 * h : start + 8 * h + 8, 128 * t : 128 * t + 128] for t in tiles}
        for h in range(groups)
    ]
    done = []
    for g in range(groups):
        lane = start % 128 + 8 * g
        rows = [
            {t: jnp.broadcast_to(x[g][t][i : i + 1, :], (8, 128)) for t in tiles} for i in range(8)
        ]
        a = {
            (u, t): jnp.broadcast_to(rows[u][own][:, lane + t : lane + t + 1], (8, 128))
            for u in range(8)
            for t in range(u + 1)
        }
        later = range(g + 1, groups)
        col = {
            (h, t): jnp.broadcast_to(x[h][own][:, lane + t : lane + t + 1], (8, 128))
            for h in later
            for t in range(8)
        }
        inverse = []
        for t in range(8):
            inverse.append(1.0 / a[t, t])
            for u in range(t + 1, 8):
                ratio = a[u, t] * inverse[t]
                for v in range(t + 1, u + 1):
                    a[u, v] = a[u, v] - ratio * a[v, t]
                for k in tiles:
                    rows[u][k] = rows[u][k] - ratio * rows[t][k]
                for h in later:
                    col[h, u] = col[h, u] - ratio * col[h, t]
        for h in later:
            for t in range(8):
                ratio = col[h, t] * inverse[t]
                for k in tiles:
                    x[h][k] = x[h][k] - ratio * rows[t][k]
        out = {}
        for t in range(8):
            guess = lax.rsqrt(a[t, t])
            scale = guess * (1.5 - 0.5 * a[t, t] * guess * guess)
            for k in tiles:
                value = rows[t][k] * scale
                out[k] = value if t == 0 else jnp.where(sub == t, value, out[k])
        for k in tiles:
            factor[start + 8 * g : start + 8 * g + 8, 128 * k : 128 * k + 128] = out[k]
        done.append(out)
    end = start + 32
    if end == KEEP:
        return
    panel = jnp.concatenate([jnp.concatenate([d[t] for t in tiles], axis=1) for d in done], axis=0)
    high, low = halves(panel)
    right = jnp.concatenate([high, high, low], axis=0)
    left = jnp.concatenate([high, low, high], axis=0)
    for t in range(own, 2):
        at = tiles.index(t) * 128
        first = max(end - 128 * t, 0)
        if first == 128:
            continue
        update = dot(left[:, at : at + 128], right, ((0,), (0,)))
        for n, k in enumerate(tiles):
            here = work[128 * t + first : 128 * t + 128, 128 * k : 128 * k + 128]
            work[128 * t + first : 128 * t + 128, 128 * k : 128 * k + 128] = (
                here - update[first:, 128 * n : 128 * n + 128]
            )


def gate_entries(left_field, right_field):
    hl = jnp.full((8, 128), left_field, F32)
    hr = jnp.full((8, 128), right_field, F32)
    half_diff = 0.5 * (hl - hr)
    width = jnp.sqrt(half_diff * half_diff + 0.25)
    factor = jnp.exp(jnp.full((8, 128), time_step * anisotropy / 4.0, F32))
    grow = jnp.exp(time_step * width)
    shrink = jnp.exp(-time_step * width)
    cosine = 0.5 * (grow + shrink)
    ratio = 0.5 * (grow - shrink) / width
    total = hl + hr
    first = jnp.exp(-time_step * (anisotropy / 4.0 + total / 2.0))
    last = jnp.exp(-time_step * (anisotropy / 4.0 - total / 2.0))
    middle = factor * (cosine - half_diff * ratio)
    other = factor * (cosine + half_diff * ratio)
    cross = -factor * ratio * 0.5
    return first, middle, cross, other, last


def kernel(
    last_ref,
    first_ref,
    start_ref,
    fields_ref,
    ranks_ref,
    left_out,
    right_out,
    right_all,
    left_all,
    mixed,
    a_rows,
    a_split,
    own_split,
    cols,
    parts,
    work,
    factor,
    prod,
    own_prod,
    left_stage,
    left_land,
    own_sem,
    pass_sem,
    r_send,
    r_recv,
    l_send,
    l_recv,
    c_send,
    c_recv,
    out_sem,
):
    seg = lax.axis_index("seg")
    bond = lax.axis_index("bond")
    z = bond // (Y * CORES)
    y = (bond // CORES) % Y
    c = bond % CORES
    owner = (seg + 7) % 8
    after = (seg + 1) % 8
    up = (y + 1) % Y
    down = (y + Y - 1) % Y
    across = (y + 2) % Y
    z_up = (z + 1) % Z
    z_down = (z + Z - 1) % Z
    z_across = (z + 2) % Z

    def place(zz, yy, cc):
        return {"bond": (zz * Y + yy) * CORES + cc}

    at_up, at_down = place(z, up, c), place(z, down, c)
    at_z_up, at_z_down = place(z_up, y, c), place(z_down, y, c)
    partner = place(z, y, 1 - c)

    barrier = pltpu.get_barrier_semaphore()
    for device in (at_up, at_down, at_z_up, at_z_down, partner, {"seg": owner}, {"seg": after}):
        pl.semaphore_signal(
            barrier, inc=1, device_id=device, device_id_type=pl.DeviceIdType.MESH
        )
    pl.semaphore_wait(barrier, 7)

    def remote(src, dst, send, recv, device):
        return pltpu.make_async_remote_copy(
            src_ref=src,
            dst_ref=dst,
            send_sem=send,
            recv_sem=recv,
            device_id=device,
            device_id_type=pl.DeviceIdType.MESH,
        )

    class SiteGather:
        def __init__(self, ref, own, send, recv):
            def copy(i, piece, device, source=None):
                return remote(piece if source is None else source, piece, send.at[i], recv.at[i], device)

            mine = ref.at[z, y, c]
            self.z_near = [copy(0, mine, at_z_up, own), copy(1, mine, at_z_down, own)]
            self.z_far = [
                copy(2, ref.at[z_down, y, c, pl.ds(0, 16)], at_z_up),
                copy(3, ref.at[z_up, y, c, pl.ds(16, 16)], at_z_down),
            ]
            order = (z, z_down, z_up, z_across)
            self.near = [
                [
                    copy(4 + 2 * j, ref.at[zz, y, c], at_up, own if j == 0 else None),
                    copy(5 + 2 * j, ref.at[zz, y, c], at_down, own if j == 0 else None),
                ]
                for j, zz in enumerate(order)
            ]
            self.far = [
                copy(12 + j, ref.at[zz, down, c], at_up)
                if j < 2
                else copy(12 + j, ref.at[zz, up, c], at_down)
                for j, zz in enumerate(order)
            ]
            self.core = [
                copy(16 + i, ref.at[:, yy, c], partner)
                for i, yy in enumerate((y, down, up, across))
            ]

        def z_first(self):
            for one in self.z_near:
                one.start()

        def y_first(self):
            for one in self.near[0]:
                one.start()

        def z_next(self):
            for one in self.z_near:
                one.wait_recv()
            for one in self.z_far:
                one.start()
            for j in (1, 2):
                for one in self.near[j]:
                    one.start()

        def z_last(self):
            for one in self.z_far:
                one.wait_recv()
            for one in self.near[3]:
                one.start()
            self.core[0].start()

        def forward(self, j):
            for one in self.near[j]:
                one.wait_recv()
            self.far[j].start()
            if j == 3:
                self.core[1].start()
                self.core[2].start()

        def across(self):
            for one in self.far:
                one.wait_recv()
            self.core[3].start()

        def drain(self):
            for one in (*self.z_near, *self.z_far, *self.far, *self.core):
                one.wait_send()
            for pair in self.near:
                for one in pair:
                    one.wait_send()

    passed = remote(last_ref.at[0], left_all.at[z, y, c], pass_sem.at[0], pass_sem.at[1], {"seg": after})
    passed.start()
    right_sites = SiteGather(right_all, first_ref.at[0], r_send, r_recv)
    left_sites = SiteGather(left_all, None, l_send, l_recv)
    right_sites.z_first()
    right_sites.y_first()
    own_copy = pltpu.make_async_copy(first_ref.at[0], right_all.at[z, y, c], own_sem)
    own_copy.start()
    passed.wait_recv()
    left_sites.z_first()
    own_copy.wait()
    right_sites.z_next()
    right_sites.z_last()
    left_sites.y_first()
    for j in range(4):
        right_sites.forward(j)
    left_sites.z_next()
    left_sites.z_last()
    right_sites.across()
    for one in right_sites.core:
        one.wait_recv()

    g_first, g_middle, g_cross, g_other, g_last = (
        g[0:1, 0:1] for g in gate_entries(fields_ref[owner, 0], fields_ref[owner, 1])
    )
    own_block = y * CORES + c
    window = pl.multiple_of(own_block * 256, 256)
    a_rows[...] = jnp.zeros_like(a_rows)

    def add_bundle(yy, cc):
        sites = left_all[:, yy, cc].reshape(128, WIDE)
        stacked = jnp.concatenate([sites[:, :CHI], sites[:, CHI:]], axis=0)

        def mix(i, carry):
            near = pl.ds(pl.multiple_of(i * 256, 256), 256)
            far = pl.ds(pl.multiple_of(CHI + i * 256, 256), 256)
            up_cols = right_all[:, :, :, :, near].reshape(CHI, 256)
            down_cols = right_all[:, :, :, :, far].reshape(CHI, 256)
            theta_up = dot(stacked, up_cols, ((1,), (0,)))
            theta_down = dot(stacked, down_cols, ((1,), (0,)))
            entries = [
                (0, near, g_first * theta_up[:128]),
                (0, far, g_middle * theta_down[:128] + g_cross * theta_up[128:]),
                (1, near, g_cross * theta_down[:128] + g_other * theta_up[128:]),
                (1, far, g_last * theta_down[128:]),
            ]
            for t, where, value in entries:
                high, low = halves(value)
                mixed[0, t, :, :, where] = high.reshape(Z, 32, 256)
                mixed[1, t, :, :, where] = low.reshape(Z, 32, 256)
            return carry

        lax.fori_loop(0, CHI // 256, mix, 0)
        high_rows = mixed[0, :, :, :, pl.ds(window, 256)].reshape(256, 256)
        low_rows = mixed[1, :, :, :, pl.ds(window, 256)].reshape(256, 256)
        both = jnp.concatenate([high_rows.T, low_rows.T], axis=0)

        def accumulate(i, carry):
            lanes = pl.ds(pl.multiple_of(i * 256, 256), 256)
            high = mixed[0, :, :, :, lanes].reshape(256, 256)
            low = mixed[1, :, :, :, lanes].reshape(256, 256)
            pair = dot(both, high, ((1,), (0,)))
            cross = dot(both[:256], low, ((1,), (0,)))
            a_rows[:, lanes] += pair[:256] + (pair[256:] + cross)
            return carry

        lax.fori_loop(0, WIDE // 256, accumulate, 0)

    add_bundle(y, c)
    for h in range(2):
        for t in range(2):
            own_split[h, 32 * t : 32 * t + 32, :] = mixed[h, t, z]
    for j in range(4):
        left_sites.forward(j)
    left_sites.core[0].wait_recv()
    add_bundle(y, 1 - c)
    add_bundle(down, c)
    left_sites.across()
    add_bundle(up, c)
    left_sites.core[1].wait_recv()
    add_bundle(down, 1 - c)
    left_sites.core[2].wait_recv()
    add_bundle(up, 1 - c)
    add_bundle(across, c)
    left_sites.core[3].wait_recv()
    add_bundle(across, 1 - c)
    passed.wait_send()
    right_sites.drain()
    left_sites.drain()

    rank = ranks_ref[owner]
    lane = lax.broadcasted_iota(jnp.int32, (1, KEEP), 1)
    used = (lane < rank).astype(F32)
    prod[...] = jnp.zeros_like(prod)

    def first_cols(i, carry):
        lines = pl.ds(pl.multiple_of(i * 256, 256), 256)
        top, rest = halves(a_rows[:, lines])
        a_split[0, :, lines] = top
        a_split[1, :, lines] = rest
        high, low = halves(start_ref[lines, :])
        prod[...] += dot(top, high, ((1,), (0,))) + (
            dot(rest, high, ((1,), (0,))) + dot(top, low, ((1,), (0,)))
        )
        return carry

    lax.fori_loop(0, WIDE // 256, first_cols, 0)
    high, low = halves(prod[...] * used)
    cols[0, y, c, 0] = high
    cols[0, y, c, 1] = low

    row_at = lax.broadcasted_iota(jnp.int32, (KEEP, KEEP), 0)
    lane_at = lax.broadcasted_iota(jnp.int32, (KEEP, KEEP), 1)
    diagonal = row_at == lane_at

    def iterate(step, carry):
        slot = step % 2

        def copy(i, piece, device):
            return remote(piece, piece, c_send.at[slot, i], c_recv.at[slot, i], device)

        def half(yy, h):
            return cols.at[slot, yy, c, h]

        near = [
            copy(0, half(y, 0), at_up),
            copy(1, half(y, 1), at_down),
            copy(2, half(y, 1), at_up),
            copy(3, half(y, 0), at_down),
        ]
        far = [copy(4, half(down, 0), at_up), copy(5, half(up, 1), at_down)]
        core = [
            copy(6, cols.at[slot, y, c], partner),
            copy(7, half(down, 0), partner),
            copy(8, half(up, 1), partner),
            copy(9, half(down, 1), partner),
            copy(10, half(up, 0), partner),
            copy(11, half(across, 0), partner),
            copy(12, half(across, 1), partner),
        ]

        def products(yy, cc):
            block = yy * CORES + cc
            high = cols[slot, yy, cc, 0]
            low = cols[slot, yy, cc, 1]
            parts[block] = dot(high, jnp.concatenate([high, low], axis=1), ((0,), (0,)))
            lanes = pl.ds(pl.multiple_of(block * 256, 256), 256)

            @pl.when(step < ITERS - 1)
            def _():
                rows = a_split[:, :, lanes].reshape(512, 256)
                pair = dot(rows, high, ((1,), (0,)))
                prod[...] += pair[:256] + (pair[256:] + dot(rows[:256], low, ((1,), (0,))))

            @pl.when(step == ITERS - 1)
            def _():
                rows = own_split[:, :, lanes].reshape(2 * ROWS, 256)
                pair = dot(rows, high, ((1,), (0,)))
                own_prod[...] += pair[:ROWS] + (
                    pair[ROWS:] + dot(rows[:ROWS], low, ((1,), (0,)))
                )

        for one in near:
            one.start()
        core[0].start()
        prod[...] = jnp.zeros_like(prod)
        own_prod[...] = jnp.zeros_like(own_prod)
        products(y, c)
        for i in range(2):
            near[i].wait_recv()
            far[i].start()
            core[1 + i].start()
        core[0].wait_recv()
        products(y, 1 - c)
        for i in range(2):
            near[2 + i].wait_recv()
            core[3 + i].start()
        products(down, c)
        products(up, c)
        for one in core[1:5]:
            one.wait_recv()
        products(down, 1 - c)
        products(up, 1 - c)
        for i in range(2):
            far[i].wait_recv()
            core[5 + i].start()
        products(across, c)
        for one in core[5:]:
            one.wait_recv()
        products(across, 1 - c)

        def total(i, carry):
            lines = pl.ds(pl.multiple_of(i * 32, 32), 32)
            value = parts[0, lines, :]
            for block in range(1, Y * CORES):
                value = value + parts[block, lines, :]
            work[lines, :] = value
            return carry

        lax.fori_loop(0, KEEP // 32, total, 0)
        unused = jnp.where(diagonal & (lane_at >= rank), 1.0, 0.0)
        cross = work[:, KEEP:]
        work[:, :KEEP] = work[:, :KEEP] + (cross + cross.T) + unused
        work[:, KEEP:] = jnp.where(diagonal, 1.0, 0.0)
        factor[...] = jnp.zeros_like(factor)
        for start in range(0, KEEP, 32):
            eliminate_panel(work, factor, start)
        for one in (*near, *far, *core):
            one.wait_send()

        @pl.when(step < ITERS - 1)
        def _():
            high, low = halves(factor[:, KEEP:])
            top, rest = halves(prod[...])
            value = dot(top, high, ((1,), (1,))) + (
                dot(top, low, ((1,), (1,))) + dot(rest, high, ((1,), (1,)))
            )
            top, rest = halves(value)
            cols[1 - slot, y, c, 0] = top
            cols[1 - slot, y, c, 1] = rest

        return carry

    lax.fori_loop(0, ITERS, iterate, 0)

    high, low = halves(factor[:, KEEP:])
    top, rest = halves(own_prod[...])
    own_prod[...] = dot(top, high, ((1,), (1,))) + (
        dot(top, low, ((1,), (1,))) + dot(rest, high, ((1,), (1,)))
    )
    for t in range(2):
        for n in range(2):
            left_stage.at[n][pl.ds(t, 32, stride=2), :] = own_prod[
                32 * t : 32 * t + 32, 128 * n : 128 * n + 128
            ]
    give = remote(left_stage, left_land, out_sem.at[0], out_sem.at[1], {"seg": owner})
    give.start()
    slot = (ITERS - 1) % 2
    inverse_high, inverse_low = halves(factor[:, KEEP:] * (float(WIDE) ** 0.5))

    def finish(i, carry):
        yy = i // CORES
        cc = i % CORES
        high = cols[slot, yy, cc, 0]
        low = cols[slot, yy, cc, 1]
        lanes = pl.ds(pl.multiple_of(i * 256, 256), 256)
        right_out[0, :, lanes] = dot(inverse_high, high, ((1,), (1,))) + (
            dot(inverse_low, high, ((1,), (1,))) + dot(inverse_high, low, ((1,), (1,)))
        )
        return carry

    lax.fori_loop(0, Y * CORES, finish, 0)
    give.wait()
    for n in range(2):
        left_out[0, :, 128 * n : 128 * n + 128] = left_land[n]


def per_device(last_sites, first_sites, start_basis, fields, ranks):
    vmem = pl.BlockSpec(memory_space=pltpu.VMEM)
    smem = pl.BlockSpec(memory_space=pltpu.SMEM)
    dma = pltpu.SemaphoreType.DMA
    return pl.pallas_call(
        kernel,
        out_shape=(
            jax.ShapeDtypeStruct((1, ROWS, KEEP), F32),
            jax.ShapeDtypeStruct((1, KEEP, WIDE), F32),
        ),
        in_specs=[vmem, vmem, vmem, smem, smem],
        out_specs=(vmem, vmem),
        scratch_shapes=[
            pltpu.VMEM((Z, Y, CORES, 32, WIDE), BF16),
            pltpu.VMEM((Z, Y, CORES, 32, WIDE), BF16),
            pltpu.VMEM((2, 2, Z, 32, WIDE), BF16),
            pltpu.VMEM((256, WIDE), F32),
            pltpu.VMEM((2, 256, WIDE), BF16),
            pltpu.VMEM((2, ROWS, WIDE), BF16),
            pltpu.VMEM((2, Y, CORES, 2, 256, KEEP), BF16),
            pltpu.VMEM((Y * CORES, KEEP, 2 * KEEP), F32),
            pltpu.VMEM((KEEP, 2 * KEEP), F32),
            pltpu.VMEM((KEEP, 2 * KEEP), F32),
            pltpu.VMEM((256, KEEP), F32),
            pltpu.VMEM((ROWS, KEEP), F32),
            pltpu.VMEM((2, ROWS, 128), F32),
            pltpu.VMEM((2, ROWS, 128), F32),
            dma,
            dma((2,)),
            dma((20,)),
            dma((20,)),
            dma((20,)),
            dma((20,)),
            dma((2, 13)),
            dma((2, 13)),
            dma((2,)),
        ],
        compiler_params=pltpu.CompilerParams(
            collective_id=0, has_side_effects=True, vmem_limit_bytes=60 * 1024 * 1024
        ),
    )(last_sites, first_sites, start_basis, fields, ranks)


def solution(mesh):
    return jax.shard_map(
        per_device,
        mesh=mesh,
        in_specs=(P("seg", "bond", None), P("seg", "bond", None), P(), P(), P()),
        out_specs=(P("seg", "bond", None), P("seg", None, None)),
        check_vma=False,
    )
```

```python
import functools

import jax
import jax.numpy as jnp
from jax import lax
from jax.experimental import pallas as pl
from jax.experimental.pallas import tpu as pltpu
from jax.sharding import PartitionSpec as P

ITERS = 4
KEEP = 256
CHI = 1024
WIDE = 2048
ROWS = 64
Z, Y, CORES = 4, 4, 2

time_step = 0.5
anisotropy = 0.6
F32 = jnp.float32
BF16 = jnp.bfloat16


def halves(x):
    high = x.astype(BF16)
    return high, (x - high.astype(F32)).astype(BF16)


def dot(a, b, dims):
    return lax.dot_general(a, b, (dims, ((), ())), preferred_element_type=F32)


def splat(x, row, lane):
    return jnp.broadcast_to(x[row : row + 1, lane : lane + 1], (8, 128))


def eliminate_panel(work, factor, start):
    own = start // 128
    tiles = list(range(own, 2)) + [2 + t for t in range(own + 1)]
    sub = lax.broadcasted_iota(jnp.int32, (8, 128), 0)
    groups = 4
    x = [
        {t: work[start + 8 * h : start + 8 * h + 8, 128 * t : 128 * t + 128] for t in tiles}
        for h in range(groups)
    ]
    done = []
    for g in range(groups):
        lane = start % 128 + 8 * g
        rows = [
            {t: jnp.broadcast_to(x[g][t][i : i + 1, :], (8, 128)) for t in tiles} for i in range(8)
        ]
        a = {
            (u, t): jnp.broadcast_to(rows[u][own][:, lane + t : lane + t + 1], (8, 128))
            for u in range(8)
            for t in range(u + 1)
        }
        later = range(g + 1, groups)
        col = {
            (h, t): jnp.broadcast_to(x[h][own][:, lane + t : lane + t + 1], (8, 128))
            for h in later
            for t in range(8)
        }
        inverse = []
        for t in range(8):
            inverse.append(1.0 / a[t, t])
            for u in range(t + 1, 8):
                ratio = a[u, t] * inverse[t]
                for v in range(t + 1, u + 1):
                    a[u, v] = a[u, v] - ratio * a[v, t]
                for k in tiles:
                    rows[u][k] = rows[u][k] - ratio * rows[t][k]
                for h in later:
                    col[h, u] = col[h, u] - ratio * col[h, t]
        for h in later:
            for t in range(8):
                ratio = col[h, t] * inverse[t]
                for k in tiles:
                    x[h][k] = x[h][k] - ratio * rows[t][k]
        out = {}
        for t in range(8):
            guess = lax.rsqrt(a[t, t])
            scale = guess * (1.5 - 0.5 * a[t, t] * guess * guess)
            for k in tiles:
                value = rows[t][k] * scale
                out[k] = value if t == 0 else jnp.where(sub == t, value, out[k])
        for k in tiles:
            factor[start + 8 * g : start + 8 * g + 8, 128 * k : 128 * k + 128] = out[k]
        done.append(out)
    end = start + 32
    if end == KEEP:
        return
    panel = jnp.concatenate([jnp.concatenate([d[t] for t in tiles], axis=1) for d in done], axis=0)
    high, low = halves(panel)
    right = jnp.concatenate([high, high, low], axis=0)
    left = jnp.concatenate([high, low, high], axis=0)
    for t in range(own, 2):
        at = tiles.index(t) * 128
        first = max(end - 128 * t, 0)
        if first == 128:
            continue
        update = dot(left[:, at : at + 128], right, ((0,), (0,)))
        for n, k in enumerate(tiles):
            here = work[128 * t + first : 128 * t + 128, 128 * k : 128 * k + 128]
            work[128 * t + first : 128 * t + 128, 128 * k : 128 * k + 128] = (
                here - update[first:, 128 * n : 128 * n + 128]
            )


def gate_entries(left_field, right_field):
    hl = jnp.full((8, 128), left_field, F32)
    hr = jnp.full((8, 128), right_field, F32)
    half_diff = 0.5 * (hl - hr)
    width = jnp.sqrt(half_diff * half_diff + 0.25)
    factor = jnp.exp(jnp.full((8, 128), time_step * anisotropy / 4.0, F32))
    grow = jnp.exp(time_step * width)
    shrink = jnp.exp(-time_step * width)
    cosine = 0.5 * (grow + shrink)
    ratio = 0.5 * (grow - shrink) / width
    total = hl + hr
    first = jnp.exp(-time_step * (anisotropy / 4.0 + total / 2.0))
    last = jnp.exp(-time_step * (anisotropy / 4.0 - total / 2.0))
    middle = factor * (cosine - half_diff * ratio)
    other = factor * (cosine + half_diff * ratio)
    cross = -factor * ratio * 0.5
    return first, middle, cross, other, last


def kernel(
    last_ref,
    first_ref,
    start_ref,
    fields_ref,
    ranks_ref,
    left_out,
    right_out,
    right_all,
    left_all,
    stacked,
    mixed,
    start_split,
    image,
    scaled,
    sent,
    landed,
    cols,
    work,
    factor,
    left_stage,
    left_land,
    own_sem,
    pass_sem,
    r_send,
    r_recv,
    l_send,
    l_recv,
    s_send,
    s_recv,
    out_sem,
):
    seg = lax.axis_index("seg")
    bond = lax.axis_index("bond")
    z = bond // (Y * CORES)
    y = (bond // CORES) % Y
    c = bond % CORES
    owner = (seg + 7) % 8
    after = (seg + 1) % 8
    up = (y + 1) % Y
    down = (y + Y - 1) % Y
    across = (y + 2) % Y
    z_up = (z + 1) % Z
    z_down = (z + Z - 1) % Z
    z_across = (z + 2) % Z

    def place(zz, yy, cc):
        return {"bond": (zz * Y + yy) * CORES + cc}

    at_up, at_down = place(z, up, c), place(z, down, c)
    at_z_up, at_z_down, at_z_across = (place(zz, y, c) for zz in (z_up, z_down, z_across))
    partner = place(z, y, 1 - c)

    barrier = pltpu.get_barrier_semaphore()
    for device in (
        at_up,
        at_down,
        at_z_up,
        at_z_down,
        at_z_across,
        partner,
        {"seg": owner},
        {"seg": after},
    ):
        pl.semaphore_signal(
            barrier, inc=1, device_id=device, device_id_type=pl.DeviceIdType.MESH
        )
    pl.semaphore_wait(barrier, 8)

    def remote(src, dst, send, recv, device):
        return pltpu.make_async_remote_copy(
            src_ref=src,
            dst_ref=dst,
            send_sem=send,
            recv_sem=recv,
            device_id=device,
            device_id_type=pl.DeviceIdType.MESH,
        )

    class SiteGather:
        def __init__(self, ref, own, send, recv, cored):
            def copy(i, piece, device, source=None):
                return remote(piece if source is None else source, piece, send.at[i], recv.at[i], device)

            def at(zz, yy, *more):
                return ref.at[(zz, yy, c, *more) if cored else (zz, yy, *more)]

            mine = at(z, y)
            self.z = [
                copy(0, mine, at_z_down, own),
                copy(1, mine, at_z_up, own),
                copy(2, mine, at_z_across, own),
            ]
            order = (z, z_up, z_down, z_across)
            self.near = [
                [
                    copy(3 + 2 * j, at(zz, y), at_up, own if j == 0 else None),
                    copy(4 + 2 * j, at(zz, y), at_down, own if j == 0 else None),
                ]
                for j, zz in enumerate(order)
            ]
            self.far = [
                [
                    copy(11 + 2 * j, at(zz, down, pl.ds(0, 16)), at_up),
                    copy(12 + 2 * j, at(zz, up, pl.ds(16, 16)), at_down),
                ]
                for j, zz in enumerate(order)
            ]
            self.core = [
                copy(19 + i, ref.at[:, yy, c], partner)
                for i, yy in enumerate((y, down, up, across) if cored else ())
            ]

        def send_z(self):
            for one in self.z:
                one.start()

        def send_y(self, j):
            if j:
                self.z[j - 1].wait_recv()
            for one in self.near[j]:
                one.start()
            if j == 3:
                for one in self.core[:1]:
                    one.start()

        def forward(self, j):
            for i in range(2):
                self.near[j][i].wait_recv()
                self.far[j][i].start()
            if j == 3:
                for one in self.core[1:3]:
                    one.start()

        def across(self):
            for pair in self.far:
                for one in pair:
                    one.wait_recv()
            for one in self.core[3:]:
                one.start()

        def drain(self):
            for one in (*self.z, *self.core):
                one.wait_send()
            for pair in (*self.near, *self.far):
                for one in pair:
                    one.wait_send()

    passed = remote(last_ref.at[0], left_all.at[z, y], pass_sem.at[0], pass_sem.at[1], {"seg": after})
    passed.start()
    right_sites = SiteGather(right_all, first_ref.at[0], r_send, r_recv, True)
    left_sites = SiteGather(left_all, None, l_send, l_recv, False)
    right_sites.send_y(0)
    right_sites.send_z()
    own_copy = pltpu.make_async_copy(first_ref.at[0], right_all.at[z, y, c], own_sem)
    own_copy.start()
    passed.wait_recv()
    left_sites.send_y(0)
    left_sites.send_z()
    own_copy.wait()

    def split_start(i, carry):
        lines = pl.ds(pl.multiple_of(i * 256, 256), 256)
        high, low = halves(start_ref[lines, :])
        start_split[0, lines, :] = high
        start_split[1, lines, :] = low
        return carry

    lax.fori_loop(0, WIDE // 256, split_start, 0)
    right_sites.forward(0)
    right_sites.send_y(1)
    right_sites.send_y(2)
    left_sites.forward(0)
    right_sites.send_y(3)
    right_sites.forward(1)
    right_sites.forward(2)
    right_sites.forward(3)
    left_sites.send_y(1)
    left_sites.send_y(2)
    left_sites.send_y(3)
    right_sites.across()
    left_sites.forward(1)
    for one in right_sites.core:
        one.wait_recv()

    g_first, g_middle, g_cross, g_other, g_last = (
        g[0:1, 0:1] for g in gate_entries(fields_ref[owner, 0], fields_ref[owner, 1])
    )
    def add_bundle(yy):
        sites = left_all[:, yy].reshape(128, WIDE)
        stacked[:128] = sites[:, :CHI]
        stacked[128:] = sites[:, CHI:]

        def mix(i, carry):
            near = pl.ds(pl.multiple_of(i * 512, 512), 512)
            far = pl.ds(pl.multiple_of(CHI + i * 512, 512), 512)
            up_cols = right_all[:, :, :, :, near].reshape(CHI, 512)
            down_cols = right_all[:, :, :, :, far].reshape(CHI, 512)
            theta_up = dot(stacked[...], up_cols, ((1,), (0,)))
            theta_down = dot(stacked[...], down_cols, ((1,), (0,)))
            entries = [
                (0, near, g_first * theta_up[:128]),
                (0, far, g_middle * theta_down[:128] + g_cross * theta_up[128:]),
                (1, near, g_cross * theta_down[:128] + g_other * theta_up[128:]),
                (1, far, g_last * theta_down[128:]),
            ]
            for t, where, value in entries:
                high, low = halves(value)
                mixed[0, yy, t, :, where] = high
                mixed[1, yy, t, :, where] = low
            return carry

        lax.fori_loop(0, CHI // 512, mix, 0)
        rows = mixed[:, yy].reshape(512, WIDE)
        pair = dot(rows, start_split[0], ((1,), (0,)))
        cross = dot(rows[:256], start_split[1], ((1,), (0,)))
        image[yy] = pair[:256] + (pair[256:] + cross)

    add_bundle(y)
    left_sites.forward(2)
    left_sites.forward(3)
    add_bundle(down)
    left_sites.across()
    add_bundle(up)
    add_bundle(across)
    passed.wait_send()
    right_sites.drain()
    left_sites.drain()

    rank = ranks_ref[owner]
    row_at = lax.broadcasted_iota(jnp.int32, (KEEP, KEEP), 0)
    lane_at = lax.broadcasted_iota(jnp.int32, (KEEP, KEEP), 1)
    diagonal = row_at == lane_at
    factor[...] = jnp.zeros_like(factor)
    factor[:, KEEP:] = jnp.where(diagonal & (lane_at < rank), 1.0, 0.0)

    def iterate(step, carry):
        slot = step % 2
        swaps = [
            remote(sent.at[n], landed.at[slot, n], s_send.at[slot, n], s_recv.at[slot, n], partner)
            for n in range(4)
        ]
        top, rest = halves(factor[:, KEEP:])
        for n in range(4):
            high, low = halves(image[n])
            value = dot(top, high, ((1,), (1,))) + (
                dot(rest, high, ((1,), (1,))) + dot(top, low, ((1,), (1,)))
            )
            high, low = halves(value)
            scaled[:256, 256 * n : 256 * n + 256] = high
            scaled[256:, 256 * n : 256 * n + 256] = low
        for n in range(4):
            high = mixed[0, :, :, :, 512 * n : 512 * n + 512].reshape(CHI, 512)
            low = mixed[1, :, :, :, 512 * n : 512 * n + 512].reshape(CHI, 512)
            pair = dot(scaled[...], high, ((1,), (0,)))
            cross = dot(scaled[:256], low, ((1,), (0,)))
            sent[n] = pair[:256] + (pair[256:] + cross)
            swaps[n].start()
        work[...] = jnp.zeros_like(work)
        for n in range(4):
            swaps[n].wait_recv()
            high, low = halves(sent[n] + landed[slot, n])
            cols[0, :, 512 * n : 512 * n + 512] = high
            cols[1, :, 512 * n : 512 * n + 512] = low
            work[...] += dot(high, jnp.concatenate([high, low], axis=0), ((1,), (1,)))
        unused = jnp.where(diagonal & (lane_at >= rank), 1.0, 0.0)
        cross = work[:, KEEP:]
        work[:, :KEEP] = work[:, :KEEP] + (cross + cross.T) + unused
        work[:, KEEP:] = jnp.where(diagonal, 1.0, 0.0)
        factor[...] = jnp.zeros_like(factor)
        for p in range(8):
            eliminate_panel(work, factor, 32 * p)
            rows = mixed[:, p // 2, p % 2].reshape(256, WIDE)
            pair = dot(rows, cols[0], ((1,), (1,)))
            cross = dot(rows[:128], cols[1], ((1,), (1,)))
            image[p // 2, 128 * (p % 2) : 128 * (p % 2) + 128, :] = pair[:128] + (pair[128:] + cross)
        for one in swaps:
            one.wait_send()
        return carry

    lax.fori_loop(0, ITERS, iterate, 0)

    top, rest = halves(factor[:, KEEP:])
    for t in range(2):
        high, low = halves(image[y, pl.ds(pl.multiple_of(128 * t + 32 * z, 32), 32), :])
        value = dot(high, top, ((1,), (1,))) + (
            dot(high, rest, ((1,), (1,))) + dot(low, top, ((1,), (1,)))
        )
        for n in range(2):
            left_stage.at[n][pl.ds(t, 32, stride=2), :] = value[:, 128 * n : 128 * n + 128]
    give = remote(left_stage, left_land, out_sem.at[0], out_sem.at[1], {"seg": owner})
    give.start()
    top, rest = halves(factor[:, KEEP:] * (float(WIDE) ** 0.5))
    for n in range(4):
        lanes = slice(512 * n, 512 * n + 512)
        right_out[0, :, lanes] = dot(top, cols[0, :, lanes], ((1,), (0,))) + (
            dot(rest, cols[0, :, lanes], ((1,), (0,))) + dot(top, cols[1, :, lanes], ((1,), (0,)))
        )
    give.wait()
    for n in range(2):
        left_out[0, :, 128 * n : 128 * n + 128] = left_land[n]


def per_device(last_sites, first_sites, start_basis, fields, ranks):
    vmem = pl.BlockSpec(memory_space=pltpu.VMEM)
    smem = pl.BlockSpec(memory_space=pltpu.SMEM)
    dma = pltpu.SemaphoreType.DMA
    return pl.pallas_call(
        kernel,
        out_shape=(
            jax.ShapeDtypeStruct((1, ROWS, KEEP), F32),
            jax.ShapeDtypeStruct((1, KEEP, WIDE), F32),
        ),
        in_specs=[vmem, vmem, vmem, smem, smem],
        out_specs=(vmem, vmem),
        scratch_shapes=[
            pltpu.VMEM((Z, Y, CORES, 32, WIDE), BF16),
            pltpu.VMEM((Z, Y, 32, WIDE), BF16),
            pltpu.VMEM((256, CHI), BF16),
            pltpu.VMEM((2, Y, 2, 128, WIDE), BF16),
            pltpu.VMEM((2, WIDE, KEEP), BF16),
            pltpu.VMEM((Y, 256, KEEP), F32),
            pltpu.VMEM((512, CHI), BF16),
            pltpu.VMEM((4, KEEP, 512), F32),
            pltpu.VMEM((2, 4, KEEP, 512), F32),
            pltpu.VMEM((2, KEEP, WIDE), BF16),
            pltpu.VMEM((KEEP, 2 * KEEP), F32),
            pltpu.VMEM((KEEP, 2 * KEEP), F32),
            pltpu.VMEM((2, ROWS, 128), F32),
            pltpu.VMEM((2, ROWS, 128), F32),
            dma,
            dma((2,)),
            dma((23,)),
            dma((23,)),
            dma((19,)),
            dma((19,)),
            dma((2, 4)),
            dma((2, 4)),
            dma((2,)),
        ],
        compiler_params=pltpu.CompilerParams(
            collective_id=0, has_side_effects=True, vmem_limit_bytes=60 * 1024 * 1024
        ),
    )(last_sites, first_sites, start_basis, fields, ranks)


def solution(mesh):
    return jax.shard_map(
        per_device,
        mesh=mesh,
        in_specs=(P("seg", "bond", None), P("seg", "bond", None), P(), P(), P()),
        out_specs=(P("seg", "bond", None), P("seg", None, None)),
        check_vma=False,
    )
```

```python
import functools

import jax
import jax.numpy as jnp
from jax import lax
from jax.experimental import pallas as pl
from jax.experimental.pallas import tpu as pltpu
from jax.sharding import PartitionSpec as P

ITERS = 4
KEEP = 256
CHI = 1024
WIDE = 2048
ROWS = 64
Z, Y, CORES = 4, 4, 2

time_step = 0.5
anisotropy = 0.6
F32 = jnp.float32
BF16 = jnp.bfloat16


def halves(x):
    high = x.astype(BF16)
    return high, (x - high.astype(F32)).astype(BF16)


def dot(a, b, dims):
    return lax.dot_general(a, b, (dims, ((), ())), preferred_element_type=F32)


def splat(x, row, lane):
    return jnp.broadcast_to(x[row : row + 1, lane : lane + 1], (8, 128))


def eliminate_panel(work, factor, start):
    own = start // 128
    tiles = list(range(own, 2)) + [2 + t for t in range(own + 1)]
    sub = lax.broadcasted_iota(jnp.int32, (8, 128), 0)
    groups = 4
    x = [
        {t: work[start + 8 * h : start + 8 * h + 8, 128 * t : 128 * t + 128] for t in tiles}
        for h in range(groups)
    ]
    done = []
    for g in range(groups):
        lane = start % 128 + 8 * g
        rows = [
            {t: jnp.broadcast_to(x[g][t][i : i + 1, :], (8, 128)) for t in tiles} for i in range(8)
        ]
        a = {
            (u, t): jnp.broadcast_to(rows[u][own][:, lane + t : lane + t + 1], (8, 128))
            for u in range(8)
            for t in range(u + 1)
        }
        later = range(g + 1, groups)
        col = {
            (h, t): jnp.broadcast_to(x[h][own][:, lane + t : lane + t + 1], (8, 128))
            for h in later
            for t in range(8)
        }
        inverse = []
        for t in range(8):
            inverse.append(1.0 / a[t, t])
            for u in range(t + 1, 8):
                ratio = a[u, t] * inverse[t]
                for v in range(t + 1, u + 1):
                    a[u, v] = a[u, v] - ratio * a[v, t]
                for k in tiles:
                    rows[u][k] = rows[u][k] - ratio * rows[t][k]
                for h in later:
                    col[h, u] = col[h, u] - ratio * col[h, t]
        for h in later:
            for t in range(8):
                ratio = col[h, t] * inverse[t]
                for k in tiles:
                    x[h][k] = x[h][k] - ratio * rows[t][k]
        out = {}
        for t in range(8):
            guess = lax.rsqrt(a[t, t])
            scale = guess * (1.5 - 0.5 * a[t, t] * guess * guess)
            for k in tiles:
                value = rows[t][k] * scale
                out[k] = value if t == 0 else jnp.where(sub == t, value, out[k])
        for k in tiles:
            factor[start + 8 * g : start + 8 * g + 8, 128 * k : 128 * k + 128] = out[k]
        done.append(out)
    end = start + 32
    if end == KEEP:
        return
    panel = jnp.concatenate([jnp.concatenate([d[t] for t in tiles], axis=1) for d in done], axis=0)
    high, low = halves(panel)
    right = jnp.concatenate([high, high, low], axis=0)
    left = jnp.concatenate([high, low, high], axis=0)
    for t in range(own, 2):
        at = tiles.index(t) * 128
        first = max(end - 128 * t, 0)
        if first == 128:
            continue
        update = dot(left[:, at : at + 128], right, ((0,), (0,)))
        for n, k in enumerate(tiles):
            here = work[128 * t + first : 128 * t + 128, 128 * k : 128 * k + 128]
            work[128 * t + first : 128 * t + 128, 128 * k : 128 * k + 128] = (
                here - update[first:, 128 * n : 128 * n + 128]
            )


def gate_entries(left_field, right_field):
    hl = jnp.full((8, 128), left_field, F32)
    hr = jnp.full((8, 128), right_field, F32)
    half_diff = 0.5 * (hl - hr)
    width = jnp.sqrt(half_diff * half_diff + 0.25)
    factor = jnp.exp(jnp.full((8, 128), time_step * anisotropy / 4.0, F32))
    grow = jnp.exp(time_step * width)
    shrink = jnp.exp(-time_step * width)
    cosine = 0.5 * (grow + shrink)
    ratio = 0.5 * (grow - shrink) / width
    total = hl + hr
    first = jnp.exp(-time_step * (anisotropy / 4.0 + total / 2.0))
    last = jnp.exp(-time_step * (anisotropy / 4.0 - total / 2.0))
    middle = factor * (cosine - half_diff * ratio)
    other = factor * (cosine + half_diff * ratio)
    cross = -factor * ratio * 0.5
    return first, middle, cross, other, last


def kernel(
    last_ref,
    first_ref,
    start_ref,
    fields_ref,
    ranks_ref,
    left_out,
    right_out,
    right_all,
    left_all,
    stacked,
    mixed,
    start_split,
    image,
    scaled,
    sent,
    landed,
    cols,
    work,
    factor,
    left_stage,
    left_land,
    own_sem,
    pass_sem,
    r_send,
    r_recv,
    l_send,
    l_recv,
    s_send,
    s_recv,
    out_sem,
    write_sem,
):
    seg = lax.axis_index("seg")
    bond = lax.axis_index("bond")
    z = bond // (Y * CORES)
    y = (bond // CORES) % Y
    c = bond % CORES
    owner = (seg + 7) % 8
    after = (seg + 1) % 8
    up = (y + 1) % Y
    down = (y + Y - 1) % Y
    across = (y + 2) % Y
    z_up = (z + 1) % Z
    z_down = (z + Z - 1) % Z
    z_across = (z + 2) % Z

    def place(zz, yy, cc):
        return {"bond": (zz * Y + yy) * CORES + cc}

    at_up, at_down = place(z, up, c), place(z, down, c)
    at_z_up, at_z_down, at_z_across = (place(zz, y, c) for zz in (z_up, z_down, z_across))
    partner = place(z, y, 1 - c)

    barrier = pltpu.get_barrier_semaphore()
    for device in (
        at_up,
        at_down,
        at_z_up,
        at_z_down,
        at_z_across,
        partner,
        {"seg": owner},
        {"seg": after},
    ):
        pl.semaphore_signal(
            barrier, inc=1, device_id=device, device_id_type=pl.DeviceIdType.MESH
        )
    pl.semaphore_wait(barrier, 8)

    def remote(src, dst, send, recv, device):
        return pltpu.make_async_remote_copy(
            src_ref=src,
            dst_ref=dst,
            send_sem=send,
            recv_sem=recv,
            device_id=device,
            device_id_type=pl.DeviceIdType.MESH,
        )

    class SiteGather:
        def __init__(self, ref, own, send, recv, cored):
            def copy(i, piece, device, source=None):
                return remote(piece if source is None else source, piece, send.at[i], recv.at[i], device)

            def at(zz, yy, *more):
                return ref.at[(zz, yy, c, *more) if cored else (zz, yy, *more)]

            mine = at(z, y)
            self.z = [
                copy(0, mine, at_z_down, own),
                copy(1, mine, at_z_up, own),
                copy(2, mine, at_z_across, own),
            ]
            order = (z, z_up, z_down, z_across)
            self.near = [
                [
                    copy(3 + 2 * j, at(zz, y), at_up, own if j == 0 else None),
                    copy(4 + 2 * j, at(zz, y), at_down, own if j == 0 else None),
                ]
                for j, zz in enumerate(order)
            ]
            self.far = [
                [
                    copy(11 + 2 * j, at(zz, down, pl.ds(0, 16)), at_up),
                    copy(12 + 2 * j, at(zz, up, pl.ds(16, 16)), at_down),
                ]
                for j, zz in enumerate(order)
            ]
            self.core = [
                copy(19 + i, ref.at[:, yy, c], partner)
                for i, yy in enumerate((y, down, up, across) if cored else ())
            ]

        def send_z(self):
            for one in self.z:
                one.start()

        def send_y(self, j):
            if j:
                self.z[j - 1].wait_recv()
            for one in self.near[j]:
                one.start()
            if j == 3:
                for one in self.core[:1]:
                    one.start()

        def forward(self, j):
            for i in range(2):
                self.near[j][i].wait_recv()
                self.far[j][i].start()
            if j == 3:
                for one in self.core[1:3]:
                    one.start()

        def across(self):
            for pair in self.far:
                for one in pair:
                    one.wait_recv()
            for one in self.core[3:]:
                one.start()

        def drain(self):
            for one in (*self.z, *self.core):
                one.wait_send()
            for pair in (*self.near, *self.far):
                for one in pair:
                    one.wait_send()

    passed = remote(last_ref.at[0], left_all.at[z, y], pass_sem.at[0], pass_sem.at[1], {"seg": after})
    passed.start()
    right_sites = SiteGather(right_all, first_ref.at[0], r_send, r_recv, True)
    left_sites = SiteGather(left_all, None, l_send, l_recv, False)
    right_sites.send_y(0)
    right_sites.send_z()
    own_copy = pltpu.make_async_copy(first_ref.at[0], right_all.at[z, y, c], own_sem)
    own_copy.start()
    passed.wait_recv()
    left_sites.send_y(0)
    left_sites.send_z()
    own_copy.wait()

    def split_start(i, carry):
        lines = pl.ds(pl.multiple_of(i * 256, 256), 256)
        high, low = halves(start_ref[lines, :])
        start_split[0, lines, :] = high
        start_split[1, lines, :] = low
        return carry

    lax.fori_loop(0, WIDE // 256, split_start, 0)
    right_sites.forward(0)
    right_sites.send_y(1)
    right_sites.send_y(2)
    left_sites.forward(0)
    right_sites.send_y(3)
    right_sites.forward(1)
    right_sites.forward(2)
    right_sites.forward(3)
    left_sites.send_y(1)
    left_sites.send_y(2)
    left_sites.send_y(3)
    right_sites.across()
    left_sites.forward(1)
    for one in right_sites.core:
        one.wait_recv()

    g_first, g_middle, g_cross, g_other, g_last = (
        g[0:1, 0:1] for g in gate_entries(fields_ref[0, owner], fields_ref[1, owner])
    )
    def add_bundle(yy):
        sites = left_all[:, yy].reshape(128, WIDE)
        stacked[:128] = sites[:, :CHI]
        stacked[128:] = sites[:, CHI:]

        def mix(i, carry):
            near = pl.ds(pl.multiple_of(i * 512, 512), 512)
            far = pl.ds(pl.multiple_of(CHI + i * 512, 512), 512)
            up_cols = right_all[:, :, :, :, near].reshape(CHI, 512)
            down_cols = right_all[:, :, :, :, far].reshape(CHI, 512)
            theta_up = dot(stacked[...], up_cols, ((1,), (0,)))
            theta_down = dot(stacked[...], down_cols, ((1,), (0,)))
            entries = [
                (0, near, g_first * theta_up[:128]),
                (0, far, g_middle * theta_down[:128] + g_cross * theta_up[128:]),
                (1, near, g_cross * theta_down[:128] + g_other * theta_up[128:]),
                (1, far, g_last * theta_down[128:]),
            ]
            for t, where, value in entries:
                high, low = halves(value)
                mixed[0, yy, t, :, where] = high
                mixed[1, yy, t, :, where] = low
            return carry

        lax.fori_loop(0, CHI // 512, mix, 0)
        rows = mixed[:, yy].reshape(512, WIDE)
        pair = dot(rows, start_split[0], ((1,), (0,)))
        cross = dot(rows[:256], start_split[1], ((1,), (0,)))
        image[yy] = pair[:256] + (pair[256:] + cross)

    add_bundle(y)
    left_sites.forward(2)
    left_sites.forward(3)
    add_bundle(down)
    left_sites.across()
    add_bundle(up)
    add_bundle(across)
    passed.wait_send()
    right_sites.drain()
    left_sites.drain()

    rank = ranks_ref[owner]
    row_at = lax.broadcasted_iota(jnp.int32, (KEEP, KEEP), 0)
    lane_at = lax.broadcasted_iota(jnp.int32, (KEEP, KEEP), 1)
    diagonal = row_at == lane_at
    factor[...] = jnp.zeros_like(factor)
    factor[:, KEEP:] = jnp.where(diagonal & (lane_at < rank), 1.0, 0.0)

    def iterate(step, carry):
        slot = step % 2
        swaps = [
            remote(sent.at[n], landed.at[slot, n], s_send.at[slot, n], s_recv.at[slot, n], partner)
            for n in range(4)
        ]
        top, rest = halves(factor[:, KEEP:])
        for n in range(4):
            high, low = halves(image[n])
            value = dot(top, high, ((1,), (1,))) + (
                dot(rest, high, ((1,), (1,))) + dot(top, low, ((1,), (1,)))
            )
            high, low = halves(value)
            scaled[:256, 256 * n : 256 * n + 256] = high
            scaled[256:, 256 * n : 256 * n + 256] = low
        for n in range(4):
            high = mixed[0, :, :, :, 512 * n : 512 * n + 512].reshape(CHI, 512)
            low = mixed[1, :, :, :, 512 * n : 512 * n + 512].reshape(CHI, 512)
            pair = dot(scaled[...], high, ((1,), (0,)))
            cross = dot(scaled[:256], low, ((1,), (0,)))
            sent[n] = pair[:256] + (pair[256:] + cross)
            swaps[n].start()
        work[...] = jnp.zeros_like(work)
        for n in range(4):
            swaps[n].wait_recv()
            high, low = halves(sent[n] + landed[slot, n])
            cols[0, :, 512 * n : 512 * n + 512] = high
            cols[1, :, 512 * n : 512 * n + 512] = low
            work[...] += dot(high, jnp.concatenate([high, low], axis=0), ((1,), (1,)))
        unused = jnp.where(diagonal & (lane_at >= rank), 1.0, 0.0)
        cross = work[:, KEEP:]
        work[:, :KEEP] = work[:, :KEEP] + (cross + cross.T) + unused
        work[:, KEEP:] = jnp.where(diagonal, 1.0, 0.0)
        factor[...] = jnp.zeros_like(factor)
        for p in range(8):
            eliminate_panel(work, factor, 32 * p)
            rows = mixed[:, p // 2, p % 2].reshape(256, WIDE)
            pair = dot(rows, cols[0], ((1,), (1,)))
            cross = dot(rows[:128], cols[1], ((1,), (1,)))
            image[p // 2, 128 * (p % 2) : 128 * (p % 2) + 128, :] = pair[:128] + (pair[128:] + cross)
        for one in swaps:
            one.wait_send()
        return carry

    lax.fori_loop(0, ITERS, iterate, 0)

    top, rest = halves(factor[:, KEEP:])
    for t in range(2):
        high, low = halves(image[y, pl.ds(pl.multiple_of(128 * t + 32 * z, 32), 32), :])
        value = dot(high, top, ((1,), (1,))) + (
            dot(high, rest, ((1,), (1,))) + dot(low, top, ((1,), (1,)))
        )
        for n in range(2):
            left_stage.at[n][pl.ds(t, 32, stride=2), :] = value[:, 128 * n : 128 * n + 128]
    give = remote(left_stage, left_land, out_sem.at[0], out_sem.at[1], {"seg": owner})
    give.start()
    top, rest = halves(factor[:, KEEP:] * (float(WIDE) ** 0.5))
    writes = []
    for n in range(4):
        lanes = slice(512 * n, 512 * n + 512)
        sent[n] = dot(top, cols[0, :, lanes], ((1,), (0,))) + (
            dot(rest, cols[0, :, lanes], ((1,), (0,))) + dot(top, cols[1, :, lanes], ((1,), (0,)))
        )
        writes.append(pltpu.make_async_copy(sent.at[n], right_out.at[0, :, lanes], write_sem.at[n]))
        writes[n].start()
    give.wait_recv()
    for n in range(2):
        lanes = slice(128 * n, 128 * n + 128)
        writes.append(pltpu.make_async_copy(left_land.at[n], left_out.at[0, :, lanes], write_sem.at[4 + n]))
        writes[4 + n].start()
    for one in writes:
        one.wait()
    give.wait_send()


def per_device(last_sites, first_sites, start_basis, fields, ranks):
    vmem = pl.BlockSpec(memory_space=pltpu.VMEM)
    smem = pl.BlockSpec(memory_space=pltpu.SMEM)
    dma = pltpu.SemaphoreType.DMA
    return pl.pallas_call(
        kernel,
        out_shape=(
            jax.ShapeDtypeStruct((1, ROWS, KEEP), F32),
            jax.ShapeDtypeStruct((1, KEEP, WIDE), F32),
        ),
        in_specs=[vmem, vmem, vmem, smem, smem],
        out_specs=(pl.BlockSpec(memory_space=pl.ANY), pl.BlockSpec(memory_space=pl.ANY)),
        scratch_shapes=[
            pltpu.VMEM((Z, Y, CORES, 32, WIDE), BF16),
            pltpu.VMEM((Z, Y, 32, WIDE), BF16),
            pltpu.VMEM((256, CHI), BF16),
            pltpu.VMEM((2, Y, 2, 128, WIDE), BF16),
            pltpu.VMEM((2, WIDE, KEEP), BF16),
            pltpu.VMEM((Y, 256, KEEP), F32),
            pltpu.VMEM((512, CHI), BF16),
            pltpu.VMEM((4, KEEP, 512), F32),
            pltpu.VMEM((2, 4, KEEP, 512), F32),
            pltpu.VMEM((2, KEEP, WIDE), BF16),
            pltpu.VMEM((KEEP, 2 * KEEP), F32),
            pltpu.VMEM((KEEP, 2 * KEEP), F32),
            pltpu.VMEM((2, ROWS, 128), F32),
            pltpu.VMEM((2, ROWS, 128), F32),
            dma,
            dma((2,)),
            dma((23,)),
            dma((23,)),
            dma((19,)),
            dma((19,)),
            dma((2, 4)),
            dma((2, 4)),
            dma((2,)),
            dma((6,)),
        ],
        compiler_params=pltpu.CompilerParams(
            collective_id=0, has_side_effects=True, vmem_limit_bytes=60 * 1024 * 1024
        ),
    )(last_sites, first_sites, start_basis, fields.T, ranks)


def solution(mesh):
    return jax.shard_map(
        per_device,
        mesh=mesh,
        in_specs=(P("seg", "bond", None), P("seg", "bond", None), P(), P(), P()),
        out_specs=(P("seg", "bond", None), P("seg", None, None)),
        check_vma=False,
    )
```

```python
import functools

import jax
import jax.numpy as jnp
from jax import lax
from jax.experimental import pallas as pl
from jax.experimental.pallas import tpu as pltpu
from jax.sharding import PartitionSpec as P

ITERS = 4
KEEP = 256
CHI = 1024
WIDE = 2048
ROWS = 64
Z, Y, CORES = 4, 4, 2

time_step = 0.5
anisotropy = 0.6
F32 = jnp.float32
BF16 = jnp.bfloat16


def halves(x):
    high = x.astype(BF16)
    return high, (x - high.astype(F32)).astype(BF16)


def dot(a, b, dims):
    return lax.dot_general(a, b, (dims, ((), ())), preferred_element_type=F32)


def splat(x, row, lane):
    return jnp.broadcast_to(x[row : row + 1, lane : lane + 1], (8, 128))


def eliminate_panel(work, factor, start):
    own = start // 128
    tiles = list(range(own, 2)) + [2 + t for t in range(own + 1)]
    sub = lax.broadcasted_iota(jnp.int32, (8, 128), 0)
    groups = 4
    x = [
        {t: work[start + 8 * h : start + 8 * h + 8, 128 * t : 128 * t + 128] for t in tiles}
        for h in range(groups)
    ]
    done = []
    for g in range(groups):
        lane = start % 128 + 8 * g
        rows = [
            {t: jnp.broadcast_to(x[g][t][i : i + 1, :], (8, 128)) for t in tiles} for i in range(8)
        ]
        a = {
            (u, t): jnp.broadcast_to(rows[u][own][:, lane + t : lane + t + 1], (8, 128))
            for u in range(8)
            for t in range(u + 1)
        }
        later = range(g + 1, groups)
        col = {
            (h, t): jnp.broadcast_to(x[h][own][:, lane + t : lane + t + 1], (8, 128))
            for h in later
            for t in range(8)
        }
        inverse = []
        for t in range(8):
            inverse.append(1.0 / a[t, t])
            for u in range(t + 1, 8):
                ratio = a[u, t] * inverse[t]
                for v in range(t + 1, u + 1):
                    a[u, v] = a[u, v] - ratio * a[v, t]
                for k in tiles:
                    rows[u][k] = rows[u][k] - ratio * rows[t][k]
                for h in later:
                    col[h, u] = col[h, u] - ratio * col[h, t]
        for h in later:
            for t in range(8):
                ratio = col[h, t] * inverse[t]
                for k in tiles:
                    x[h][k] = x[h][k] - ratio * rows[t][k]
        out = {}
        for t in range(8):
            guess = lax.rsqrt(a[t, t])
            scale = guess * (1.5 - 0.5 * a[t, t] * guess * guess)
            for k in tiles:
                value = rows[t][k] * scale
                out[k] = value if t == 0 else jnp.where(sub == t, value, out[k])
        for k in tiles:
            factor[start + 8 * g : start + 8 * g + 8, 128 * k : 128 * k + 128] = out[k]
        done.append(out)
    end = start + 32
    if end == KEEP:
        return
    panel = jnp.concatenate([jnp.concatenate([d[t] for t in tiles], axis=1) for d in done], axis=0)
    high, low = halves(panel)
    right = jnp.concatenate([high, high, low], axis=0)
    left = jnp.concatenate([high, low, high], axis=0)
    for t in range(own, 2):
        at = tiles.index(t) * 128
        first = max(end - 128 * t, 0)
        if first == 128:
            continue
        update = dot(left[:, at : at + 128], right, ((0,), (0,)))
        for n, k in enumerate(tiles):
            here = work[128 * t + first : 128 * t + 128, 128 * k : 128 * k + 128]
            work[128 * t + first : 128 * t + 128, 128 * k : 128 * k + 128] = (
                here - update[first:, 128 * n : 128 * n + 128]
            )


def gate_entries(left_field, right_field):
    hl = jnp.full((8, 128), left_field, F32)
    hr = jnp.full((8, 128), right_field, F32)
    half_diff = 0.5 * (hl - hr)
    width = jnp.sqrt(half_diff * half_diff + 0.25)
    factor = jnp.exp(jnp.full((8, 128), time_step * anisotropy / 4.0, F32))
    grow = jnp.exp(time_step * width)
    shrink = jnp.exp(-time_step * width)
    cosine = 0.5 * (grow + shrink)
    ratio = 0.5 * (grow - shrink) / width
    total = hl + hr
    first = jnp.exp(-time_step * (anisotropy / 4.0 + total / 2.0))
    last = jnp.exp(-time_step * (anisotropy / 4.0 - total / 2.0))
    middle = factor * (cosine - half_diff * ratio)
    other = factor * (cosine + half_diff * ratio)
    cross = -factor * ratio * 0.5
    return first, middle, cross, other, last


def kernel(
    last_ref,
    first_ref,
    start_ref,
    fields_ref,
    ranks_ref,
    left_out,
    right_out,
    right_all,
    left_all,
    stacked,
    mixed,
    start_split,
    image,
    scaled,
    sent,
    landed,
    cols,
    work,
    factor,
    left_stage,
    left_land,
    own_sem,
    pass_sem,
    r_send,
    r_recv,
    l_send,
    l_recv,
    s_send,
    s_recv,
    out_sem,
    write_sem,
):
    seg = lax.axis_index("seg")
    bond = lax.axis_index("bond")
    z = bond // (Y * CORES)
    y = (bond // CORES) % Y
    c = bond % CORES
    owner = (seg + 7) % 8
    after = (seg + 1) % 8
    up = (y + 1) % Y
    down = (y + Y - 1) % Y
    across = (y + 2) % Y
    z_up = (z + 1) % Z
    z_down = (z + Z - 1) % Z
    z_across = (z + 2) % Z

    def place(zz, yy, cc):
        return {"bond": (zz * Y + yy) * CORES + cc}

    at_up, at_down = place(z, up, c), place(z, down, c)
    at_z_up, at_z_down, at_z_across = (place(zz, y, c) for zz in (z_up, z_down, z_across))
    partner = place(z, y, 1 - c)

    barrier = pltpu.get_barrier_semaphore()
    for device in (
        at_up,
        at_down,
        at_z_up,
        at_z_down,
        at_z_across,
        partner,
        {"seg": owner},
        {"seg": after},
    ):
        pl.semaphore_signal(
            barrier, inc=1, device_id=device, device_id_type=pl.DeviceIdType.MESH
        )
    pl.semaphore_wait(barrier, 8)

    def remote(src, dst, send, recv, device):
        return pltpu.make_async_remote_copy(
            src_ref=src,
            dst_ref=dst,
            send_sem=send,
            recv_sem=recv,
            device_id=device,
            device_id_type=pl.DeviceIdType.MESH,
        )

    class SiteGather:
        def __init__(self, ref, own, send, recv, cored):
            def copy(i, piece, device, source=None):
                return remote(piece if source is None else source, piece, send.at[i], recv.at[i], device)

            def at(zz, yy, *more):
                return ref.at[(zz, yy, c, *more) if cored else (zz, yy, *more)]

            mine = at(z, y)
            self.z = [
                copy(0, mine, at_z_down, own),
                copy(1, mine, at_z_up, own),
                copy(2, mine, at_z_across, own),
            ]
            order = (z, z_up, z_down, z_across)
            self.near = [
                [
                    copy(3 + 2 * j, at(zz, y), at_up, own if j == 0 else None),
                    copy(4 + 2 * j, at(zz, y), at_down, own if j == 0 else None),
                ]
                for j, zz in enumerate(order)
            ]
            self.far = [
                [
                    copy(11 + 2 * j, at(zz, down, pl.ds(0, 16)), at_up),
                    copy(12 + 2 * j, at(zz, up, pl.ds(16, 16)), at_down),
                ]
                for j, zz in enumerate(order)
            ]
            self.core = [
                copy(19 + i, ref.at[:, yy, c], partner)
                for i, yy in enumerate((y, down, up, across) if cored else ())
            ]

        def send_z(self):
            for one in self.z:
                one.start()

        def send_y(self, j):
            if j:
                self.z[j - 1].wait_recv()
            for one in self.near[j]:
                one.start()
            if j == 3:
                for one in self.core[:1]:
                    one.start()

        def forward(self, j):
            for i in range(2):
                self.near[j][i].wait_recv()
                self.far[j][i].start()
            if j == 3:
                for one in self.core[1:3]:
                    one.start()

        def across(self):
            for pair in self.far:
                for one in pair:
                    one.wait_recv()
            for one in self.core[3:]:
                one.start()

        def drain(self):
            for one in (*self.z, *self.core):
                one.wait_send()
            for pair in (*self.near, *self.far):
                for one in pair:
                    one.wait_send()

    passed = remote(last_ref.at[0], left_all.at[z, y], pass_sem.at[0], pass_sem.at[1], {"seg": after})
    passed.start()
    right_sites = SiteGather(right_all, first_ref.at[0], r_send, r_recv, True)
    left_sites = SiteGather(left_all, None, l_send, l_recv, False)
    right_sites.send_y(0)
    right_sites.send_z()
    own_copy = pltpu.make_async_copy(first_ref.at[0], right_all.at[z, y, c], own_sem)
    own_copy.start()
    passed.wait_recv()
    left_sites.send_y(0)
    left_sites.send_z()
    own_copy.wait()

    def split_start(i, carry):
        lines = pl.ds(pl.multiple_of(i * 256, 256), 256)
        high, low = halves(start_ref[lines, :])
        start_split[0, lines, :] = high
        start_split[1, lines, :] = low
        return carry

    lax.fori_loop(0, WIDE // 256, split_start, 0)
    right_sites.forward(0)
    right_sites.send_y(1)
    right_sites.send_y(2)
    left_sites.forward(0)
    right_sites.send_y(3)
    right_sites.forward(1)
    right_sites.forward(2)
    right_sites.forward(3)
    left_sites.send_y(1)
    left_sites.send_y(2)
    left_sites.send_y(3)
    right_sites.across()
    left_sites.forward(1)
    for one in right_sites.core:
        one.wait_recv()

    g_first, g_middle, g_cross, g_other, g_last = (
        g[0:1, 0:1] for g in gate_entries(fields_ref[0, owner], fields_ref[1, owner])
    )
    def add_bundle(yy):
        sites = left_all[:, yy].reshape(128, WIDE)
        stacked[:128] = sites[:, :CHI]
        stacked[128:] = sites[:, CHI:]

        def mix(i, carry):
            near = pl.ds(pl.multiple_of(i * 512, 512), 512)
            far = pl.ds(pl.multiple_of(CHI + i * 512, 512), 512)
            up_cols = right_all[:, :, :, :, near].reshape(CHI, 512)
            down_cols = right_all[:, :, :, :, far].reshape(CHI, 512)
            theta_up = dot(stacked[...], up_cols, ((1,), (0,)))
            theta_down = dot(stacked[...], down_cols, ((1,), (0,)))
            entries = [
                (0, near, g_first * theta_up[:128]),
                (0, far, g_middle * theta_down[:128] + g_cross * theta_up[128:]),
                (1, near, g_cross * theta_down[:128] + g_other * theta_up[128:]),
                (1, far, g_last * theta_down[128:]),
            ]
            for t, where, value in entries:
                high, low = halves(value)
                mixed[0, yy, t, :, where] = high
                mixed[1, yy, t, :, where] = low
            return carry

        lax.fori_loop(0, CHI // 512, mix, 0)
        rows = mixed[:, yy].reshape(512, WIDE)
        pair = dot(rows, start_split[0], ((1,), (0,)))
        cross = dot(rows[:256], start_split[1], ((1,), (0,)))
        image[yy] = pair[:256] + (pair[256:] + cross)

    add_bundle(y)
    left_sites.forward(2)
    left_sites.forward(3)
    add_bundle(down)
    left_sites.across()
    add_bundle(up)
    add_bundle(across)
    passed.wait_send()
    right_sites.drain()
    left_sites.drain()

    rank = ranks_ref[owner]
    row_at = lax.broadcasted_iota(jnp.int32, (KEEP, KEEP), 0)
    lane_at = lax.broadcasted_iota(jnp.int32, (KEEP, KEEP), 1)
    diagonal = row_at == lane_at
    factor[...] = jnp.zeros_like(factor)
    factor[:, KEEP:] = jnp.where(diagonal & (lane_at < rank), 1.0, 0.0)

    def iterate(step, carry):
        slot = step % 2
        swaps = [
            remote(sent.at[n], landed.at[slot, n], s_send.at[slot, n], s_recv.at[slot, n], partner)
            for n in range(4)
        ]
        top, rest = halves(factor[:, KEEP:])
        for n in range(4):
            high, low = halves(image[n])
            value = dot(top, high, ((1,), (1,))) + (
                dot(rest, high, ((1,), (1,))) + dot(top, low, ((1,), (1,)))
            )
            high, low = halves(value)
            scaled[:256, 256 * n : 256 * n + 256] = high
            scaled[256:, 256 * n : 256 * n + 256] = low
        for n in range(4):
            high = mixed[0, :, :, :, 512 * n : 512 * n + 512].reshape(CHI, 512)
            low = mixed[1, :, :, :, 512 * n : 512 * n + 512].reshape(CHI, 512)
            pair = dot(scaled[...], high, ((1,), (0,)))
            cross = dot(scaled[:256], low, ((1,), (0,)))
            sent[n] = pair[:256] + (pair[256:] + cross)
            swaps[n].start()
        work[...] = jnp.zeros_like(work)
        for n in range(4):
            swaps[n].wait_recv()
            high, low = halves(sent[n] + landed[slot, n])
            cols[0, :, 512 * n : 512 * n + 512] = high
            cols[1, :, 512 * n : 512 * n + 512] = low
            work[...] += dot(high, jnp.concatenate([high, low], axis=0), ((1,), (1,)))
        unused = jnp.where(diagonal & (lane_at >= rank), 1.0, 0.0)
        cross = work[:, KEEP:]
        work[:, :KEEP] = work[:, :KEEP] + (cross + cross.T) + unused
        work[:, KEEP:] = jnp.where(diagonal, 1.0, 0.0)
        factor[...] = jnp.zeros_like(factor)
        for p in range(8):
            rows = mixed[:, p // 2, p % 2].reshape(256, WIDE)
            pair = dot(rows, cols[0], ((1,), (1,)))
            cross = dot(rows[:128], cols[1], ((1,), (1,)))
            image[p // 2, 128 * (p % 2) : 128 * (p % 2) + 128, :] = pair[:128] + (pair[128:] + cross)
            eliminate_panel(work, factor, 32 * p)
        for one in swaps:
            one.wait_send()
        return carry

    lax.fori_loop(0, ITERS, iterate, 0)

    top, rest = halves(factor[:, KEEP:])
    for t in range(2):
        high, low = halves(image[y, pl.ds(pl.multiple_of(128 * t + 32 * z, 32), 32), :])
        value = dot(high, top, ((1,), (1,))) + (
            dot(high, rest, ((1,), (1,))) + dot(low, top, ((1,), (1,)))
        )
        for n in range(2):
            left_stage.at[n][pl.ds(t, 32, stride=2), :] = value[:, 128 * n : 128 * n + 128]
    give = remote(left_stage, left_land, out_sem.at[0], out_sem.at[1], {"seg": owner})
    give.start()
    top, rest = halves(factor[:, KEEP:] * (float(WIDE) ** 0.5))
    writes = []
    for n in range(4):
        lanes = slice(512 * n, 512 * n + 512)
        sent[n] = dot(top, cols[0, :, lanes], ((1,), (0,))) + (
            dot(rest, cols[0, :, lanes], ((1,), (0,))) + dot(top, cols[1, :, lanes], ((1,), (0,)))
        )
        writes.append(pltpu.make_async_copy(sent.at[n], right_out.at[0, :, lanes], write_sem.at[n]))
        writes[n].start()
    give.wait_recv()
    for n in range(2):
        lanes = slice(128 * n, 128 * n + 128)
        writes.append(pltpu.make_async_copy(left_land.at[n], left_out.at[0, :, lanes], write_sem.at[4 + n]))
        writes[4 + n].start()
    for one in writes:
        one.wait()
    give.wait_send()


def per_device(last_sites, first_sites, start_basis, fields, ranks):
    vmem = pl.BlockSpec(memory_space=pltpu.VMEM)
    smem = pl.BlockSpec(memory_space=pltpu.SMEM)
    dma = pltpu.SemaphoreType.DMA
    return pl.pallas_call(
        kernel,
        out_shape=(
            jax.ShapeDtypeStruct((1, ROWS, KEEP), F32),
            jax.ShapeDtypeStruct((1, KEEP, WIDE), F32),
        ),
        in_specs=[vmem, vmem, vmem, smem, smem],
        out_specs=(pl.BlockSpec(memory_space=pl.ANY), pl.BlockSpec(memory_space=pl.ANY)),
        scratch_shapes=[
            pltpu.VMEM((Z, Y, CORES, 32, WIDE), BF16),
            pltpu.VMEM((Z, Y, 32, WIDE), BF16),
            pltpu.VMEM((256, CHI), BF16),
            pltpu.VMEM((2, Y, 2, 128, WIDE), BF16),
            pltpu.VMEM((2, WIDE, KEEP), BF16),
            pltpu.VMEM((Y, 256, KEEP), F32),
            pltpu.VMEM((512, CHI), BF16),
            pltpu.VMEM((4, KEEP, 512), F32),
            pltpu.VMEM((2, 4, KEEP, 512), F32),
            pltpu.VMEM((2, KEEP, WIDE), BF16),
            pltpu.VMEM((KEEP, 2 * KEEP), F32),
            pltpu.VMEM((KEEP, 2 * KEEP), F32),
            pltpu.VMEM((2, ROWS, 128), F32),
            pltpu.VMEM((2, ROWS, 128), F32),
            dma,
            dma((2,)),
            dma((23,)),
            dma((23,)),
            dma((19,)),
            dma((19,)),
            dma((2, 4)),
            dma((2, 4)),
            dma((2,)),
            dma((6,)),
        ],
        compiler_params=pltpu.CompilerParams(
            collective_id=0, has_side_effects=True, vmem_limit_bytes=60 * 1024 * 1024
        ),
    )(last_sites, first_sites, start_basis, fields.T, ranks)


def solution(mesh):
    return jax.shard_map(
        per_device,
        mesh=mesh,
        in_specs=(P("seg", "bond", None), P("seg", "bond", None), P(), P(), P()),
        out_specs=(P("seg", "bond", None), P("seg", None, None)),
        check_vma=False,
    )
```
